128 devices in a mesh: tm: 16 (over y, x), row: 4 (over z), col: 2 (over core).
Axes of the slice: x: 4, y: 4, z: 4, core: 2. Of those that a mesh axis runs over, the one named last changes fastest.
Arguments:
- blocks: float32 [16, 4096, 4096], P('tm', 'row', 'col'), may hold values from -0.7 to 7.7, as said below
- borders: float32 [16, 640, 4096], P('tm', None, ('row', 'col')), may hold values from -0.3 to 0.3
- arrow_tip: float32 [128, 128], replicated, may hold values from -6 to 6
Outputs:
- schur_blocks: float32 [16, 4096, 4096], P('tm', 'row', 'col')
- factor_panels: float32 [16, 4096, 1024], P('tm', 'row')
- border_out: float32 [16, 640, 4096], P('tm', None, ('row', 'col'))
- tip_out: float32 [128, 128], replicated
The draws below stay inside these ranges and needn't reach their ends.
Inputs may be any that keep to these rules, and one draw needn't show every extreme that they name: `blocks`: each partition's block is symmetric positive definite.
All inputs are finite; a program needn't handle non-finite values.
Results may differ from the reference program's by a relative error of at most 0.0001.
Values sent between devices are 32-bit elements; how exact they have to be, the bound alone decides.
No kernel may reach another device: no remote copies, remote signals or barrier semaphores. Data moves between devices by JAX's collectives and lax.ppermute only.
A program may use at most 128 MiB of HBM per device.

```python
import math
import jax
import jax.numpy as jnp
from jax import lax

NODES = 4096
F = 128
P_SIZE = 512
Q = 512
PANELS = 2
PARTITIONS = 16
N_ROW = 4


def draw_blocks(key, part):
    keys = jax.random.split(key, 2)
    noise = jnp.clip(jax.random.normal(keys[0], (PARTITIONS, NODES, NODES), jnp.float32), -5.0, 5.0)
    diag = jax.random.uniform(keys[1], (PARTITIONS, NODES), jnp.float32, 3.0, 6.0)
    noise = (noise + jnp.swapaxes(noise, 1, 2)) * (0.7071068 / math.sqrt(NODES))
    return noise + diag[:, :, None] * jnp.eye(NODES, dtype=jnp.float32)[None]


def shard_levels(own_key, shape, pieces, least, largest):
    factor_of = 1.0
    for position, blocks in pieces:
        heights = jax.random.uniform(jax.random.fold_in(jax.random.fold_in(own_key, 6), position), (blocks,), jnp.float32, least / len(pieces), largest / len(pieces))
        factor_of = factor_of * jnp.repeat(jnp.exp(heights), shape[position] // blocks).reshape((-1,) + (1,) * (len(shape) - 1 - position))
    return factor_of


def gaussian(own_key, dims, scale, most, cuts=(), kind=jnp.bfloat16):
    result = scale * jax.random.normal(own_key, dims, jnp.float32)
    if cuts:
        result = result * shard_levels(own_key, dims, cuts, -0.22, 0.18)
    return jnp.clip(result, -most, most).astype(kind)


def setup_inputs(seed: int = 0) -> dict:
    key_of = jax.random.split(jax.random.key(seed), 4)
    return {
        "blocks": draw_blocks(jax.random.fold_in(key_of[3], 71), 0),
        "borders": gaussian(key_of[1], (PARTITIONS, Q + F, NODES), 0.05, 0.3, ((0, 16), (2, 8)), jnp.float32),
        "arrow_tip": gaussian(key_of[2], (F, F), 1.0, 6.0, (), jnp.float32),
    }


def exact_dot(left, right):
    return jnp.dot(left.astype(jnp.float32), right.astype(jnp.float32), precision=lax.Precision.HIGHEST, preferred_element_type=jnp.float32)

def right_solve(chol, values):
    return lax.linalg.triangular_solve(chol, values, left_side=False, lower=True, transpose_a=True)

def panel_nodes(k):
    slice_width = P_SIZE // N_ROW
    starts = jnp.arange(N_ROW, dtype=jnp.int32)[:, None] * (NODES // N_ROW) + k * slice_width
    return (starts + jnp.arange(slice_width, dtype=jnp.int32)[None, :]).reshape(-1)

def one_partition(inputs):
    block, border = inputs
    offsets = jnp.arange(NODES, dtype=jnp.int32) % (NODES // N_ROW)
    handoff = jnp.zeros((Q + F, Q), jnp.float32)
    tip_term = jnp.zeros((F, F), jnp.float32)
    factors = []
    for k in range(PANELS):
        nodes = panel_nodes(k)
        panel = jnp.take(block, nodes, axis=1)
        corner = jnp.take(panel, nodes, axis=0)
        chol = jnp.linalg.cholesky(corner)
        rows = right_solve(chol, panel)
        rows = jnp.where((offsets < k * (P_SIZE // N_ROW))[:, None], jnp.float32(0.0), rows)
        arrow = right_solve(chol, jnp.take(border, nodes, axis=1))
        block = block - exact_dot(rows, rows.T)
        border = border - exact_dot(arrow, rows.T)
        handoff = handoff + exact_dot(arrow, arrow[:Q].T)
        tip_term = tip_term + exact_dot(arrow[Q:], arrow[Q:].T)
        factors.append(rows)
    return (block, jnp.concatenate(factors, axis=1), border, handoff, tip_term)

def reference(blocks, borders, arrow_tip):
    new_blocks, factors, new_borders, handoffs, tip_terms = lax.map(one_partition, (blocks, borders))
    received = jnp.concatenate([jnp.zeros((1, Q + F, Q), jnp.float32), handoffs[:-1]], axis=0)
    new_blocks = new_blocks.at[:, NODES - Q:, NODES - Q:].add(-received[:, :Q])
    new_borders = new_borders.at[:, Q:, NODES - Q:].add(-received[:, Q:])
    tip_out = arrow_tip - jnp.sum(tip_terms, axis=0)
    return (new_blocks, factors, new_borders, tip_out)
```

```python
import functools

import jax
import jax.numpy as jnp
from jax import lax
from jax.experimental import pallas as pl
from jax.experimental.pallas import tpu as pltpu
from jax.sharding import PartitionSpec as P

F = 128
PANEL = 512
Q = 512
B = 128
N = 1024
ROWS = 4
F32 = jnp.float32
BF16 = jnp.bfloat16
HIGHEST = lax.Precision.HIGHEST
NN = ((1,), (0,))
NT = ((1,), (1,))
TN = ((0,), (0,))


def dot(left, right, dims, precision=HIGHEST):
    return lax.dot_general(left, right, (dims, ((), ())), precision=precision, preferred_element_type=F32)


def split(value):
    high = value.astype(BF16)
    return high, (value - high.astype(F32)).astype(BF16)


def dot3(left_high, left_low, right_high, right_low, dims):
    one = lambda a, b: lax.dot_general(a, b, (dims, ((), ())), preferred_element_type=F32)
    return one(left_high, right_high) + (one(left_high, right_low) + one(left_low, right_high))


def factor_rows(rows, base, lane, sub):
    count = len(rows)
    done = []
    for g in range(count):
        first = base + 8 * g
        cols = {h: [jnp.broadcast_to(rows[h][:, first + i : first + i + 1], (8, B)) for i in range(8)] for h in range(g, count)}
        tri = {(a, b): jnp.broadcast_to(cols[g][b][a : a + 1, :], (8, B)) for b in range(8) for a in range(b, 8)}
        row = [jnp.broadcast_to(rows[g][a : a + 1, :], (8, B)) for a in range(8)]
        final = None
        fac = {}
        for i in range(8):
            scale = lax.rsqrt(tri[i, i])
            for a in range(i + 1, 8):
                fac[a, i] = tri[a, i] * scale
            for b in range(i + 1, 8):
                for a in range(b, 8):
                    tri[a, b] = tri[a, b] - fac[a, i] * fac[b, i]
            pivot = lane == (first + i)
            unit = row[i] * scale
            both = jnp.where(pivot, unit + scale, unit)
            packed = jnp.where(pivot, scale, unit)
            final = packed if final is None else jnp.where(sub == i, packed, final)
            for a in range(i + 1, 8):
                row[a] = row[a] - fac[a, i] * both
            for h in range(g + 1, count):
                ratio = cols[h][i] * scale
                for b in range(i + 1, 8):
                    cols[h][b] = cols[h][b] - ratio * fac[b, i]
                rows[h] = rows[h] - ratio * both
        done.append(final)
    return done


def factor_tile(tile, step=32):
    lane = lax.broadcasted_iota(jnp.int32, (8, B), 1)
    sub = lax.broadcasted_iota(jnp.int32, (8, B), 0)
    lane_q = lax.broadcasted_iota(jnp.int32, (step, B), 1)
    sub_q = lax.broadcasted_iota(jnp.int32, (step, B), 0)
    lane_t = lax.broadcasted_iota(jnp.int32, (B, B), 1)
    for base in range(0, B, step):
        rows = [tile[base + 8 * h : base + 8 * h + 8, :] for h in range(step // 8)]
        final = jnp.concatenate(factor_rows(rows, base, lane, sub), axis=0)
        tile[base : base + step, :] = final
        end = base + step
        if end < B:
            left = jnp.where(lane_q >= end, final, 0.0)
            right = jnp.where((lane_q > sub_q + base) & (lane_q < end), 0.0, final)
            update = dot(left, right, TN)
            keep = (lane_t[end:] >= end) | (lane_t[end:] < base)
            tile[end:, :] = jnp.where(keep, tile[end:, :], 0.0) - update[end:, :]


def inverse_factor(square, inverse, tile):
    size = square.shape[0]
    sub_b = lax.broadcasted_iota(jnp.int32, (B, B), 0)
    lane_b = lax.broadcasted_iota(jnp.int32, (B, B), 1)
    sub_n = lax.broadcasted_iota(jnp.int32, (B, size), 0)
    lane_n = lax.broadcasted_iota(jnp.int32, (B, size), 1)

    def body(j, carry):
        first = pl.multiple_of(j * B, B)
        here = pl.ds(first, B)
        tile[...] = square[here, here]
        factor_tile(tile)
        corner = jnp.where(lane_b <= sub_b, tile[...], 0.0)
        square[here, here] = jnp.where(lane_b == sub_b, 1.0, 0.0)
        row = dot(corner, square[here, :], NN)
        inverse[here, :] = jnp.where(lane_n <= sub_n + first, row, 0.0)
        left = jnp.where(lane_n >= first + B, row, 0.0)
        square[:, here] = jnp.zeros((size, B), F32)
        square[...] = square[...] - dot(left, row, TN)
        return carry

    lax.fori_loop(0, size // B, body, 0)


def first_corner_kernel(place, *refs):
    mine, theirs = refs[0:4], refs[4:8]
    corner, inverse, square, tile = refs[8:]
    row, col = place[0], place[1]
    for d in range(ROWS):
        at = pl.ds(pl.multiple_of(((row + ROWS - d) & 3) * B, B), B)
        corner[at, pl.ds(pl.multiple_of(col * 256, 256), 256)] = mine[d][...]
        corner[at, pl.ds(pl.multiple_of((1 - col) * 256, 256), 256)] = theirs[d][...]
    square[...] = corner[...]
    inverse_factor(square, inverse, tile)


def second_corner_kernel(place, *refs):
    mine, theirs = refs[0:4], refs[4:8]
    first_inverse, corner, high, low, square, inverse, tile = refs[8:]
    row, col = place[0], place[1]
    for d in range(ROWS):
        at = pl.ds(pl.multiple_of(((row + ROWS - d) & 3) * B, B), B)
        for k in range(2):
            corner[at, pl.ds(pl.multiple_of(k * PANEL + col * 256, 256), 256)] = mine[d][:, k * 256 : (k + 1) * 256]
            corner[at, pl.ds(pl.multiple_of(k * PANEL + (1 - col) * 256, 256), 256)] = theirs[d][:, k * 256 : (k + 1) * 256]
    w00 = first_inverse[...]
    c10 = dot(corner[:, :PANEL], w00, NT)
    square[...] = corner[:, PANEL:] - dot(c10, c10, NT)
    inverse_factor(square, inverse, tile)
    w11 = inverse[...]
    w10 = -dot(w11, dot(c10, w00, NN), NN)
    high[:PANEL, :PANEL], low[:PANEL, :PANEL] = split(w00)
    high[PANEL:, :PANEL], low[PANEL:, :PANEL] = split(w10)
    high[PANEL:, PANEL:], low[PANEL:, PANEL:] = split(w11)
    high[:PANEL, PANEL:] = jnp.zeros((PANEL, PANEL), BF16)
    low[:PANEL, PANEL:] = jnp.zeros((PANEL, PANEL), BF16)


def border_kernel(place, *refs):
    pieces = refs[0:4]
    w_high, w_low, y_high, y_low, handoff, tip, b_high, b_low = refs[4:]
    row = place[0]
    for d in range(ROWS):
        source = (row + ROWS - d) & 3
        for k in range(2):
            at = pl.ds(pl.multiple_of(k * PANEL + source * B, B), B)
            b_high[:, at], b_low[:, at] = split(pieces[d][:, k * B : (k + 1) * B])
    for k, width in ((0, PANEL), (1, N)):
        out = slice(k * PANEL, (k + 1) * PANEL)
        part = dot3(b_high[:, :width], b_low[:, :width], w_high[out, :width], w_low[out, :width], NT)
        y_high[:, out], y_low[:, out] = split(part)
    tip[...] = dot3(y_high[Q:, :], y_low[Q:, :], y_high[Q:, :], y_low[Q:, :], NT)
    handoff[...] = dot3(y_high[...], y_low[...], y_high[:Q, :], y_low[:Q, :], NT)


def factor_kernel(place, own, other, w_high, w_low, y_high, y_low, border, factor, l_high, l_low, border_out, p_high, p_low):
    step = pl.program_id(0)
    col = place[1]
    size = own.shape[0]

    @pl.when(step < ROWS)
    def _():
        for k in range(2):
            at = pl.ds(pl.multiple_of(k * PANEL + col * 256, 256), 256)
            p_high[:, at], p_low[:, at] = split(own[:, k * 256 : (k + 1) * 256])
            at = pl.ds(pl.multiple_of(k * PANEL + (1 - col) * 256, 256), 256)
            p_high[:, at], p_low[:, at] = split(other[:, k * 256 : (k + 1) * 256])
        node = lax.broadcasted_iota(jnp.int32, (size, PANEL), 0) + step * size
        rows = pl.ds(pl.multiple_of(step * size, size), size)
        for k, width in ((0, PANEL), (1, N)):
            out = slice(k * PANEL, (k + 1) * PANEL)
            part = dot3(p_high[:, :width], p_low[:, :width], w_high[out, :width], w_low[out, :width], NT)
            if k:
                part = jnp.where(node < B, 0.0, part)
            factor[:, out] = part
            l_high[rows, out], l_low[rows, out] = split(part)

    @pl.when(step == ROWS)
    def _():
        nodes = pl.ds(pl.multiple_of(col * PANEL, PANEL), PANEL)
        border_out[...] = border[...] - dot3(y_high[...], y_low[...], l_high[nodes, :], l_low[nodes, :], NT)


def update_kernel(place, block, top, g1, g2, g3, m0, m1, w_high, w_low, l_high, l_low, *refs, half):
    if half:
        incoming, _, out, r_high, r_low, v_high, v_low = refs
    else:
        out, r_high, r_low, v_high, v_low = refs
    step = pl.program_id(0)
    row, col = place[0], place[1]
    node_block = 2 * col + half
    size = block.shape[0]
    mine = node_block == row

    @pl.when(jnp.logical_and(step == 0, jnp.logical_not(mine)))
    def _():
        near = pl.ds(pl.multiple_of(node_block * B, B), B)
        r_high[:PANEL, :B], r_low[:PANEL, :B] = split(m0[:, near])
        r_high[:PANEL, B : 2 * B], r_low[:PANEL, B : 2 * B] = split(m1[near, :PANEL].T)
        r_high[PANEL:, :B], r_low[PANEL:, :B] = split(m1[:, near])
        near = pl.ds(pl.multiple_of(PANEL + node_block * B, B), B)
        r_high[PANEL:, B : 2 * B], r_low[PANEL:, B : 2 * B] = split(m1[:, near])
        for d, piece in enumerate((None, g1, g2, g3)):
            source = (row + ROWS - d) & 3
            for k in range(2):
                at = pl.ds(pl.multiple_of(k * PANEL + source * B, B), B)
                rows = slice(k * B, (k + 1) * B)
                value = top[rows, 2 * B :] if piece is None else piece[rows, :]
                r_high[at, 2 * B :], r_low[at, 2 * B :] = split(value)
        node = lax.broadcasted_iota(jnp.int32, (256, N), 1)
        for t in range(4):
            rows = slice(t * 256, (t + 1) * 256)
            width = (t + 1) * 256
            part = dot3(w_high[rows, :width], w_low[rows, :width], r_high[:width, :], r_low[:width, :], NN)
            if t >= 2:
                part = jnp.where(node < B, 0.0, part)
            v_high[rows, :], v_low[rows, :] = split(part)

    rows = pl.ds(pl.multiple_of(step * size, size), size)

    @pl.when(mine)
    def _():
        out[...] = block[...] - dot3(l_high[rows, :], l_low[rows, :], l_high[...], l_low[...], NT)

    @pl.when(jnp.logical_not(mine))
    def _():
        out[...] = block[...] - dot3(l_high[rows, :], l_low[rows, :], v_high[...], v_low[...], NN)

    if half:

        @pl.when(step * size >= N - Q)
        def _():
            out[:, N - Q :] = out[:, N - Q :] - incoming[...]


VMEM = pl.BlockSpec(memory_space=pltpu.VMEM)


def limits(mib):
    return pltpu.CompilerParams(vmem_limit_bytes=mib << 20)


def whole(shape):
    return pl.BlockSpec(shape, lambda i, *_: (0,) * len(shape))


def struct(shape, dtype=F32):
    return jax.ShapeDtypeStruct(shape, dtype)


def shards(blocks, borders, arrow_tip):
    block = blocks[0]
    border = borders[0]
    row = lax.axis_index("row")
    col = lax.axis_index("col")
    place = jnp.stack([row, col]).astype(jnp.int32)

    def along_row(value, shift):
        return lax.ppermute(value, "row", [(s, (s + shift) % ROWS) for s in range(ROWS)])

    def to_other(value):
        return lax.ppermute(value, "col", [(0, 1), (1, 0)])

    def pick(rows, ks):
        return jnp.concatenate([block[rows, h * N + k * B : h * N + (k + 1) * B] for k in ks for h in range(2)], axis=1)

    def spread(value):
        mine = [value] + [along_row(value, d) for d in (1, 2, 3)]
        return mine, [to_other(v) for v in mine]

    first_mine, first_theirs = spread(pick(slice(0, B), (0,)))
    second_mine, second_theirs = spread(pick(slice(B, 2 * B), (0, 1)))
    own = pick(slice(None), (0, 1))
    other = to_other(own)

    edge = border[:, : 2 * B]
    edges = []
    for d in range(ROWS):
        near = edge
        if d:
            near = lax.ppermute(edge, ("row", "col"), [(2 * s, 2 * ((s + d) % ROWS)) for s in range(ROWS)])
        far = lax.ppermute(near, "col", [(0, 1)])
        edges.append(jnp.where(col == 0, near, far))

    bulk = {}
    for h in range(2):
        part = block[: 2 * B, h * N + 2 * B : (h + 1) * N]
        for d in (1, 3, 2):
            pairs = []
            for s in range(ROWS):
                for c in range(2):
                    t = (s + d) % ROWS
                    if t != 2 * c + h:
                        pairs.append((2 * s + c, 2 * t + c))
            bulk[h, d] = lax.ppermute(part, ("row", "col"), pairs)

    def grid(count, ins, outs, scratch=(), steps=()):
        return pltpu.PrefetchScalarGridSpec(
            num_scalar_prefetch=count, grid=steps, in_specs=ins, out_specs=outs, scratch_shapes=list(scratch)
        )

    m0, w00 = pl.pallas_call(
        first_corner_kernel,
        grid_spec=grid(1, [VMEM] * 8, [VMEM] * 2, [pltpu.VMEM((PANEL, PANEL), F32), pltpu.VMEM((B, B), F32)]),
        out_shape=[struct((PANEL, PANEL)), struct((PANEL, PANEL))],
        compiler_params=limits(16),
        name="first_corner",
    )(place, *first_mine, *first_theirs)

    m1, w_high, w_low = pl.pallas_call(
        second_corner_kernel,
        grid_spec=grid(
            1,
            [VMEM] * 9,
            [VMEM] * 3,
            [pltpu.VMEM((PANEL, PANEL), F32), pltpu.VMEM((PANEL, PANEL), F32), pltpu.VMEM((B, B), F32)],
        ),
        out_shape=[struct((PANEL, N)), struct((N, N), BF16), struct((N, N), BF16)],
        compiler_params=limits(24),
        name="second_corner",
    )(place, *second_mine, *second_theirs, w00)

    edge_rows = border.shape[0]
    y_high, y_low, handoff, tip = pl.pallas_call(
        border_kernel,
        grid_spec=grid(1, [VMEM] * 6, [VMEM] * 4, [pltpu.VMEM((edge_rows, N), BF16)] * 2),
        out_shape=[struct((edge_rows, N), BF16), struct((edge_rows, N), BF16), struct((edge_rows, Q)), struct((F, F))],
        compiler_params=limits(40),
        name="border_rows",
    )(place, *edges, w_high, w_low)

    count = lax.axis_size("tm")
    last = 2 * ROWS - 1
    incoming = lax.ppermute(
        handoff, ("tm", "row", "col"), [(t * 2 * ROWS + last, (t + 1) * 2 * ROWS + last) for t in range(count - 1)]
    )
    shift = 1
    while shift < count:
        tip = tip + lax.ppermute(tip, "tm", [(t, t ^ shift) for t in range(count)])
        shift *= 2
    tip_out = arrow_tip - tip

    tile = N // ROWS
    clamp = lambda i, *_: (jnp.minimum(i, ROWS - 1), 0)
    factor, l_high, l_low, border_out = pl.pallas_call(
        factor_kernel,
        grid_spec=grid(
            1,
            [
                pl.BlockSpec((tile, PANEL), clamp),
                pl.BlockSpec((tile, PANEL), clamp),
                whole((N, N)),
                whole((N, N)),
                whole((edge_rows, N)),
                whole((edge_rows, N)),
                whole((edge_rows, PANEL)),
            ],
            [pl.BlockSpec((tile, N), clamp), whole((N, N)), whole((N, N)), whole((edge_rows, PANEL))],
            [pltpu.VMEM((tile, N), BF16)] * 2,
            (ROWS + 1,),
        ),
        out_shape=[struct((N, N)), struct((N, N), BF16), struct((N, N), BF16), struct((edge_rows, PANEL))],
        compiler_params=limits(48),
        name="factor_rows",
    )(place, own, other, w_high, w_low, y_high, y_low, border)
    border_out = border_out.at[Q:].add(-incoming[Q:])

    schur = None
    for h in range(2):
        extra, extra_specs, aliases = [], [], {}
        if h:
            extra = [incoming, schur]
            extra_specs = [pl.BlockSpec((tile, Q), lambda i, *_: (jnp.maximum(i - 2, 0), 0)), pl.BlockSpec(memory_space=pl.ANY)]
            aliases = {13: 0}
        schur = pl.pallas_call(
            functools.partial(update_kernel, half=h),
            grid_spec=grid(
                1,
                [
                    pl.BlockSpec((tile, N), lambda i, *_, h=h: (i, h)),
                    pl.BlockSpec((2 * B, N), lambda i, *_, h=h: (0, h)),
                    whole((2 * B, N - 2 * B)),
                    whole((2 * B, N - 2 * B)),
                    whole((2 * B, N - 2 * B)),
                    whole((PANEL, PANEL)),
                    whole((PANEL, N)),
                    whole((N, N)),
                    whole((N, N)),
                    whole((N, N)),
                    whole((N, N)),
                ]
                + extra_specs,
                pl.BlockSpec((tile, N), lambda i, *_, h=h: (i, h)),
                [pltpu.VMEM((N, N), BF16)] * 4,
                (ROWS,),
            ),
            out_shape=struct(block.shape),
            input_output_aliases=aliases,
            compiler_params=limits(58),
            name="update_%d" % h,
        )(place, block, block, bulk[h, 1], bulk[h, 2], bulk[h, 3], m0, m1, w_high, w_low, l_high, l_low, *extra)

    return schur[None], factor[None], border_out[None], tip_out


def solution(mesh):
    return jax.shard_map(
        shards,
        mesh=mesh,
        in_specs=(P("tm", "row", "col"), P("tm", None, ("row", "col")), P()),
        out_specs=(P("tm", "row", "col"), P("tm", "row", None), P("tm", None, ("row", "col")), P()),
        check_vma=False,
    )
```

```python
import functools

import jax
import jax.numpy as jnp
from jax import lax
from jax.experimental import pallas as pl
from jax.experimental.pallas import tpu as pltpu
from jax.sharding import PartitionSpec as P


F = 128
PANEL = 512
Q = 512
B = 128
N = 1024
ROWS = 4
F32 = jnp.float32
BF16 = jnp.bfloat16
HIGHEST = lax.Precision.HIGHEST
NN = ((1,), (0,))
NT = ((1,), (1,))
TN = ((0,), (0,))


def dot(left, right, dims, precision=HIGHEST):
    return lax.dot_general(left, right, (dims, ((), ())), precision=precision, preferred_element_type=F32)


def split(value):
    high = value.astype(BF16)
    return high, (value - high.astype(F32)).astype(BF16)


def dot3(left_high, left_low, right_high, right_low, dims):
    one = lambda a, b: lax.dot_general(a, b, (dims, ((), ())), preferred_element_type=F32)
    return one(left_high, right_high) + (one(left_high, right_low) + one(left_low, right_high))


def factor_rows(rows, base, lane, sub):
    count = len(rows)
    done = []
    for g in range(count):
        first = base + 8 * g
        cols = {h: [jnp.broadcast_to(rows[h][:, first + i : first + i + 1], (8, B)) for i in range(8)] for h in range(g, count)}
        tri = {(a, b): jnp.broadcast_to(cols[g][b][a : a + 1, :], (8, B)) for b in range(8) for a in range(b, 8)}
        row = [jnp.broadcast_to(rows[g][a : a + 1, :], (8, B)) for a in range(8)]
        final = None
        fac = {}
        for i in range(8):
            scale = lax.rsqrt(tri[i, i])
            for a in range(i + 1, 8):
                fac[a, i] = tri[a, i] * scale
            for b in range(i + 1, 8):
                for a in range(b, 8):
                    tri[a, b] = tri[a, b] - fac[a, i] * fac[b, i]
            pivot = lane == (first + i)
            unit = row[i] * scale
            both = jnp.where(pivot, unit + scale, unit)
            packed = jnp.where(pivot, scale, unit)
            final = packed if final is None else jnp.where(sub == i, packed, final)
            for a in range(i + 1, 8):
                row[a] = row[a] - fac[a, i] * both
            for h in range(g + 1, count):
                ratio = cols[h][i] * scale
                for b in range(i + 1, 8):
                    cols[h][b] = cols[h][b] - ratio * fac[b, i]
                rows[h] = rows[h] - ratio * both
        done.append(final)
    return done


def factor_tile(tile, step=32):
    lane = lax.broadcasted_iota(jnp.int32, (8, B), 1)
    sub = lax.broadcasted_iota(jnp.int32, (8, B), 0)
    lane_q = lax.broadcasted_iota(jnp.int32, (step, B), 1)
    sub_q = lax.broadcasted_iota(jnp.int32, (step, B), 0)
    lane_t = lax.broadcasted_iota(jnp.int32, (B, B), 1)
    for base in range(0, B, step):
        rows = [tile[base + 8 * h : base + 8 * h + 8, :] for h in range(step // 8)]
        final = jnp.concatenate(factor_rows(rows, base, lane, sub), axis=0)
        tile[base : base + step, :] = final
        end = base + step
        if end < B:
            left = jnp.where(lane_q >= end, final, 0.0)
            right = jnp.where((lane_q > sub_q + base) & (lane_q < end), 0.0, final)
            update = dot(left, right, TN)
            keep = (lane_t[end:] >= end) | (lane_t[end:] < base)
            tile[end:, :] = jnp.where(keep, tile[end:, :], 0.0) - update[end:, :]


def inverse_factor(square, inverse, tile):
    size = square.shape[0]
    sub_b = lax.broadcasted_iota(jnp.int32, (B, B), 0)
    lane_b = lax.broadcasted_iota(jnp.int32, (B, B), 1)
    sub_n = lax.broadcasted_iota(jnp.int32, (B, size), 0)
    lane_n = lax.broadcasted_iota(jnp.int32, (B, size), 1)

    def body(j, carry):
        first = pl.multiple_of(j * B, B)
        here = pl.ds(first, B)
        tile[...] = square[here, here]
        factor_tile(tile)
        corner = jnp.where(lane_b <= sub_b, tile[...], 0.0)
        square[here, here] = jnp.where(lane_b == sub_b, 1.0, 0.0)
        row = dot(corner, square[here, :], NN)
        inverse[here, :] = jnp.where(lane_n <= sub_n + first, row, 0.0)
        left = jnp.where(lane_n >= first + B, row, 0.0)
        square[:, here] = jnp.zeros((size, B), F32)
        square[...] = square[...] - dot(left, row, TN)
        return carry

    lax.fori_loop(0, size // B, body, 0)


def first_corner_kernel(place, *refs):
    mine, theirs = refs[0:4], refs[4:8]
    corner, inverse, square, tile = refs[8:]
    row, col = place[0], place[1]
    for d in range(ROWS):
        at = pl.ds(pl.multiple_of(((row + ROWS - d) & 3) * B, B), B)
        corner[at, pl.ds(pl.multiple_of(col * 256, 256), 256)] = mine[d][...]
        corner[at, pl.ds(pl.multiple_of((1 - col) * 256, 256), 256)] = theirs[d][...]
    square[...] = corner[...]
    inverse_factor(square, inverse, tile)


def second_corner_kernel(place, *refs):
    mine, theirs = refs[0:4], refs[4:8]
    first_inverse, corner, high, low, square, inverse, tile = refs[8:]
    row, col = place[0], place[1]
    for d in range(ROWS):
        at = pl.ds(pl.multiple_of(((row + ROWS - d) & 3) * B, B), B)
        for k in range(2):
            corner[at, pl.ds(pl.multiple_of(k * PANEL + col * 256, 256), 256)] = mine[d][k * B : (k + 1) * B, :]
            corner[at, pl.ds(pl.multiple_of(k * PANEL + (1 - col) * 256, 256), 256)] = theirs[d][k * B : (k + 1) * B, :]
    w00 = first_inverse[...]
    c10 = dot(corner[:, :PANEL], w00, NT)
    square[...] = corner[:, PANEL:] - dot(c10, c10, NT)
    inverse_factor(square, inverse, tile)
    w11 = inverse[...]
    w10 = -dot(w11, dot(c10, w00, NN), NN)
    high[:PANEL, :PANEL], low[:PANEL, :PANEL] = split(w00)
    high[PANEL:, :PANEL], low[PANEL:, :PANEL] = split(w10)
    high[PANEL:, PANEL:], low[PANEL:, PANEL:] = split(w11)
    high[:PANEL, PANEL:] = jnp.zeros((PANEL, PANEL), BF16)
    low[:PANEL, PANEL:] = jnp.zeros((PANEL, PANEL), BF16)


def border_kernel(place, *refs):
    mine, theirs = refs[0:4], refs[4:8]
    w_high, w_low, y_high, y_low, handoff, tip, b_high, b_low = refs[8:]
    row, col = place[0], place[1]
    count = mine[0].shape[0] - 2 * B
    for d in range(ROWS):
        source = (row + ROWS - d) & 3
        for owner, piece in ((col, mine[d]), (1 - col, theirs[d])):
            rows = pl.ds(pl.multiple_of(owner * count, 64), count)
            for k in range(2):
                at = pl.ds(pl.multiple_of(k * PANEL + source * B, B), B)
                b_high[rows, at], b_low[rows, at] = split(piece[2 * B :, k * B : (k + 1) * B])
    for k, width in ((0, PANEL), (1, N)):
        out = slice(k * PANEL, (k + 1) * PANEL)
        part = dot3(b_high[:, :width], b_low[:, :width], w_high[out, :width], w_low[out, :width], NT)
        y_high[:, out], y_low[:, out] = split(part)
    tip[...] = dot3(y_high[Q:, :], y_low[Q:, :], y_high[Q:, :], y_low[Q:, :], NT)
    handoff[...] = dot3(y_high[...], y_low[...], y_high[:Q, :], y_low[:Q, :], NT)


def factor_kernel(place, own0, own1, other0, other1, w_high, w_low, factor, l_high, l_low, p_high, p_low):
    step = pl.program_id(0)
    col = place[1]
    size = own0.shape[0]
    for owner, pieces in ((col, (own0, own1)), (1 - col, (other0, other1))):
        for h in range(2):
            for k in range(2):
                at = pl.ds(pl.multiple_of(k * PANEL + (2 * owner + h) * B, B), B)
                p_high[:, at], p_low[:, at] = split(pieces[h][:, k * B : (k + 1) * B])
    node = lax.broadcasted_iota(jnp.int32, (size, PANEL), 0) + step * size
    rows = pl.ds(pl.multiple_of(step * size, size), size)
    for k, width in ((0, PANEL), (1, N)):
        out = slice(k * PANEL, (k + 1) * PANEL)
        part = dot3(p_high[:, :width], p_low[:, :width], w_high[out, :width], w_low[out, :width], NT)
        if k:
            part = jnp.where(node < B, 0.0, part)
        factor[:, out] = part
        l_high[rows, out], l_low[rows, out] = split(part)


def border_out_kernel(place, border, y_high, y_low, l_high, l_low, incoming, _, out):
    nodes = pl.ds(pl.multiple_of(place[1] * PANEL, PANEL), PANEL)
    out[...] = border[...] - dot3(y_high[...], y_low[...], l_high[nodes, :], l_low[nodes, :], NT)
    out[Q:, :] = out[Q:, :] - incoming[Q:, :]


def update_kernel(place, block, top, near, far, passed, m0, m1, w_high, w_low, l_high, l_low, *refs, half):
    if half:
        incoming, _, _, out, r_high, r_low, v_high, v_low = refs
    else:
        out, token, r_high, r_low, v_high, v_low = refs
        token[...] = jnp.zeros_like(token)
    step = pl.program_id(0)
    row, col = place[0], place[1]
    node_block = 2 * col + half
    size = block.shape[0]
    mine = node_block == row
    wide = N - 2 * B

    @pl.when(jnp.logical_and(step == 0, jnp.logical_not(mine)))
    def _():
        at = pl.ds(pl.multiple_of(node_block * B, B), B)
        r_high[:PANEL, :B], r_low[:PANEL, :B] = split(m0[:, at])
        r_high[:PANEL, B : 2 * B], r_low[:PANEL, B : 2 * B] = split(m1[at, :PANEL].T)
        r_high[PANEL:, :B], r_low[PANEL:, :B] = split(m1[:, at])
        at = pl.ds(pl.multiple_of(PANEL + node_block * B, B), B)
        r_high[PANEL:, B : 2 * B], r_low[PANEL:, B : 2 * B] = split(m1[:, at])
        for d in range(ROWS):
            source = (row + ROWS - d) & 3
            for k in range(2):
                at = pl.ds(pl.multiple_of(k * PANEL + source * B, B), B)
                rows = slice(k * B, (k + 1) * B)
                if d == 0:
                    value = top[rows, 2 * B :]
                elif d == 2:
                    value = passed[rows, :]
                else:
                    value = (near if d == 1 else far)[rows, half * wide : (half + 1) * wide]
                r_high[at, 2 * B :], r_low[at, 2 * B :] = split(value)
        node = lax.broadcasted_iota(jnp.int32, (256, N), 1)
        for t in range(4):
            rows = slice(t * 256, (t + 1) * 256)
            width = (t + 1) * 256
            part = dot3(w_high[rows, :width], w_low[rows, :width], r_high[:width, :], r_low[:width, :], NN)
            if t >= 2:
                part = jnp.where(node < B, 0.0, part)
            v_high[rows, :], v_low[rows, :] = split(part)

    rows = pl.ds(pl.multiple_of(step * size, size), size)

    @pl.when(mine)
    def _():
        out[...] = block[...] - dot3(l_high[rows, :], l_low[rows, :], l_high[...], l_low[...], NT)

    @pl.when(jnp.logical_not(mine))
    def _():
        out[...] = block[...] - dot3(l_high[rows, :], l_low[rows, :], v_high[...], v_low[...], NN)

    if half:

        @pl.when(step * size >= N - Q)
        def _():
            at = pl.ds(pl.multiple_of(jnp.maximum(step * size - (N - Q), 0), size), size)
            out[:, N - Q :] = out[:, N - Q :] - incoming[at, :]


VMEM = pl.BlockSpec(memory_space=pltpu.VMEM)


def limits(mib):
    return pltpu.CompilerParams(vmem_limit_bytes=mib << 20)


def struct(shape, dtype=F32):
    return jax.ShapeDtypeStruct(shape, dtype)


def step(blocks, borders, arrow_tip):
    block = blocks[0]
    border = borders[0]
    row = lax.axis_index("row")
    col = lax.axis_index("col")
    place = jnp.stack([row, col]).astype(jnp.int32)
    edge_rows = border.shape[0]

    def along_row(value, shift):
        return lax.ppermute(value, "row", [(s, (s + shift) % ROWS) for s in range(ROWS)])

    def to_other(value):
        return lax.ppermute(value, "col", [(0, 1), (1, 0)])

    def spread(value):
        mine = [value, *(along_row(value, d) for d in (1, 2, 3))]
        return mine, [to_other(v) for v in mine]

    def pick(rows, k):
        return [block[rows, h * N + k * B : h * N + (k + 1) * B] for h in range(2)]

    first_mine, first_theirs = spread(jnp.concatenate(pick(slice(0, B), 0), axis=1))
    lower = lax.ppermute(border[edge_rows // 2 :, : 2 * B], "col", [(0, 1)])
    edge = jnp.where(col == 0, border[: edge_rows // 2, : 2 * B], lower)
    low_rows = [jnp.concatenate(pick(slice(B, 2 * B), k), axis=1) for k in range(2)]
    second_mine, second_theirs = spread(jnp.concatenate([*low_rows, edge], axis=0))

    others = [to_other(block[:, h * N : h * N + 2 * B]) for h in range(2)]

    wide = N - 2 * B
    bulk = jnp.concatenate([block[: 2 * B, h * N + 2 * B : (h + 1) * N] for h in range(2)], axis=1)
    near = along_row(bulk, 1)
    far = along_row(bulk, 3)
    passed = [along_row(near[:, :wide], 1), along_row(far[:, wide:], 3)]

    def grid(ins, outs, scratch=(), steps=()):
        return pltpu.PrefetchScalarGridSpec(
            num_scalar_prefetch=1, grid=steps, in_specs=ins, out_specs=outs, scratch_shapes=list(scratch)
        )

    def call(kernel, mib, spec, out, *args, **more):
        return pl.pallas_call(kernel, grid_spec=spec, out_shape=out, compiler_params=limits(mib), **more)(place, *args)

    square = pltpu.VMEM((PANEL, PANEL), F32)
    m0, w00 = call(
        first_corner_kernel,
        8,
        grid([VMEM] * 8, [VMEM] * 2, [square, pltpu.VMEM((B, B), F32)]),
        [struct((PANEL, PANEL)), struct((PANEL, PANEL))],
        *first_mine,
        *first_theirs,
    )
    m1, w_high, w_low = call(
        second_corner_kernel,
        14,
        grid([VMEM] * 9, [VMEM] * 3, [square, square, pltpu.VMEM((B, B), F32)]),
        [struct((PANEL, N)), struct((N, N), BF16), struct((N, N), BF16)],
        *second_mine,
        *second_theirs,
        w00,
    )
    y_high, y_low, handoff, tip = call(
        border_kernel,
        22,
        grid([VMEM] * 10, [VMEM] * 4, [pltpu.VMEM((edge_rows, N), BF16)] * 2),
        [struct((edge_rows, N), BF16), struct((edge_rows, N), BF16), struct((edge_rows, Q)), struct((F, F))],
        *second_mine,
        *second_theirs,
        w_high,
        w_low,
    )

    count = lax.axis_size("tm")
    last = 2 * ROWS - 1
    incoming = lax.ppermute(
        handoff, ("tm", "row", "col"), [(t * 2 * ROWS + last, (t + 1) * 2 * ROWS + last) for t in range(count - 1)]
    )
    for mask in (1, 3, 4, 12):
        tip = tip + lax.ppermute(tip, "tm", [(t, t ^ mask) for t in range(count)])
    tip_out = arrow_tip - tip

    tile = N // ROWS
    piece = lambda j: pl.BlockSpec((tile, 2 * B), lambda i, *_: (i, j))
    factor, l_high, l_low = call(
        factor_kernel,
        20,
        grid(
            [piece(0), piece(4), piece(0), piece(0), VMEM, VMEM],
            [pl.BlockSpec((tile, N), lambda i, *_: (i, 0)), VMEM, VMEM],
            [pltpu.VMEM((tile, N), BF16)] * 2,
            (ROWS,),
        ),
        [struct((N, N)), struct((N, N), BF16), struct((N, N), BF16)],
        block,
        block,
        *others,
        w_high,
        w_low,
    )

    schur = None
    for h in range(2):
        ins = [
            pl.BlockSpec((tile, N), lambda i, *_, h=h: (i, h)),
            pl.BlockSpec((2 * B, N), lambda i, *_, h=h: (0, h)),
        ] + [VMEM] * 9
        outs = pl.BlockSpec((tile, N), lambda i, *_, h=h: (i, h))
        out = struct(block.shape)
        args = [block, block, near, far, passed[h], m0, m1, w_high, w_low, l_high, l_low]
        more = {}
        if h:
            ins += [VMEM, pl.BlockSpec(memory_space=pl.ANY), pl.BlockSpec(memory_space=pl.ANY)]
            args += [incoming, schur, border_out]
            more = {"input_output_aliases": {13: 0}}
        else:
            outs = [outs, VMEM]
            out = [out, struct((8, B))]
        schur = call(
            functools.partial(update_kernel, half=h),
            28,
            grid(ins, outs, [pltpu.VMEM((N, N), BF16)] * 4, (ROWS,)),
            out,
            *args,
            **more,
        )
        if not h:
            schur, token = schur
            border_out = call(
                border_out_kernel,
                14,
                grid([VMEM] * 6 + [pl.BlockSpec(memory_space=pl.ANY)], VMEM),
                struct(border.shape),
                border,
                y_high,
                y_low,
                l_high,
                l_low,
                incoming,
                token,
            )

    return schur[None], factor[None], border_out[None], tip_out


def solution(mesh):
    return jax.shard_map(
        step,
        mesh=mesh,
        in_specs=(P("tm", "row", "col"), P("tm", None, ("row", "col")), P()),
        out_specs=(P("tm", "row", "col"), P("tm", "row", None), P("tm", None, ("row", "col")), P()),
        check_vma=False,
    )
```
